32 devices in a mesh: dp: 16 (over z, x, core), tensor: 2 (over y).
Axes of the slice: x: 2, y: 2, z: 4, core: 2. Of those that a mesh axis runs over, the one named last changes fastest.
Arguments:
- tokens: bfloat16 [4096, 8192], P('dp', 'tensor'), may hold values from -6 to 6
- out_grad: bfloat16 [4096, 2, 256], P('dp', 'tensor'), may hold values from -2 to 2
- active: int32 [16, 2, 2], P('dp', 'tensor'), may hold values from 0 to 112, as said below
- w_gate: bfloat16 [8192, 28672], P('dp', 'tensor'), may hold values from -0.0625 to 0.0625
- w_up: bfloat16 [8192, 28672], P('dp', 'tensor'), may hold values from -0.0625 to 0.0625
Outputs:
- input_grad: bfloat16 [4096, 8192], P('dp', 'tensor')
- gate_weight_grad: bfloat16 [8192, 28672], P('dp', 'tensor')
- up_weight_grad: bfloat16 [8192, 28672], P('dp', 'tensor')
The draws below stay inside these ranges and needn't reach their ends.
Inputs may be any that keep to these rules, and one draw needn't show every extreme that they name: `active`: each entry is a block number of the shard or 112 for an empty slot. In every tile and shard the live entries come first, are distinct and number at least one; in every tile some shard has all 2 slots live.
All inputs are finite; a program needn't handle non-finite values.
Results may differ from the reference program's by a relative error of at most 0.014.
Values may be sent and summed in bfloat16 or wider, within the bound.
No kernel may reach another device: no remote copies, remote signals or barrier semaphores. Data moves between devices by JAX's collectives and lax.ppermute only.
A program may use at most 128 MiB of HBM per device.

```python
import jax
import jax.numpy as jnp
from jax import lax

D = 8192
FF = 28672
BLOCK = 128
TILE = 256
CAP = 2
SHARDS = 2
BPS = 112
TILES = 16
TOKENS = 4096


def draw_active(key, part):
    key_scores, key_counts, key_full = jax.random.split(key, 3)
    scores = jax.random.randint(key_scores, (TILES, SHARDS, BPS), 0, 1 << 20) * BPS + jnp.arange(BPS, dtype=jnp.int32)
    chosen = jnp.sort(jnp.argsort(scores, axis=-1)[..., :CAP], axis=-1).astype(jnp.int32)
    counts = jax.random.randint(key_counts, (TILES, SHARDS), 1, CAP + 1)
    full_shard = jax.random.randint(key_full, (TILES,), 0, SHARDS)
    counts = jnp.where(jnp.arange(SHARDS)[None, :] == full_shard[:, None], CAP, counts)
    slot_index = jnp.arange(CAP)[None, None, :]
    return jnp.where(slot_index < counts[..., None], chosen, BPS).astype(jnp.int32)


def levels(rng, extent, shards, least, largest):
    gain, own = 1.0, jax.random.fold_in(rng, 6)
    for axis_at, blocks in shards:
        heights = jnp.exp(jax.random.uniform(jax.random.fold_in(own, axis_at), (blocks,), jnp.float32, least / len(shards), largest / len(shards)))
        gain = gain * jnp.repeat(heights, extent[axis_at] // blocks).reshape([-1 if axis == axis_at else 1 for axis in range(len(extent))])
    return gain


def scatter_about(stream_key, extent, deviation, bound, pieces=(), held_as=jnp.bfloat16):
    values = jax.random.normal(stream_key, extent, jnp.float32) * deviation
    if len(pieces) > 0:
        values = levels(stream_key, extent, pieces, -0.22, 0.18) * values
    return jnp.clip(values, min=-bound, max=bound).astype(held_as)


def setup_inputs(seed: int = 0) -> dict:
    keys = jax.random.split(jax.random.key(seed), 6)
    return {
        "tokens": scatter_about(keys[0], (TOKENS, D), 1.0, 6.0, ((0, 16), (1, 2))),
        "out_grad": scatter_about(keys[1], (TOKENS, SHARDS, CAP * BLOCK), 0.3, 2.0, ((0, 16), (1, 2))),
        "active": draw_active(jax.random.fold_in(keys[5], 71), 0),
        "w_gate": scatter_about(keys[3], (D, FF), D ** -0.5, 0.0625, ((0, 16), (1, 2))),
        "w_up": scatter_about(keys[4], (D, FF), D ** -0.5, 0.0625, ((0, 16), (1, 2))),
    }


def reference(tokens, out_grad, active, w_gate, w_up):
    gate_shaped = w_gate.reshape(D, SHARDS, BPS, BLOCK)
    up_shaped = w_up.reshape(D, SHARDS, BPS, BLOCK)
    shard_ids = jnp.arange(SHARDS).astype(jnp.int32)[:, None]
    unit_ids = jnp.arange(BLOCK).astype(jnp.int32)

    def one_tile(carry, inputs):
        gate_total, up_total = carry
        tile_rows, tile_grad, tile_active = inputs
        alive = (tile_active < BPS).astype(jnp.float32)
        picked = jnp.minimum(tile_active, BPS - 1).astype(jnp.int32)
        gate_cols = gate_shaped[:, shard_ids, picked]
        up_cols = up_shaped[:, shard_ids, picked]
        gate_flat = gate_cols.reshape(D, SHARDS * CAP * BLOCK)
        up_flat = up_cols.reshape(D, SHARDS * CAP * BLOCK)
        gate_value = jnp.dot(tile_rows, gate_flat, preferred_element_type=jnp.float32).reshape(TILE, SHARDS, CAP, BLOCK)
        up_value = jnp.dot(tile_rows, up_flat, preferred_element_type=jnp.float32).reshape(TILE, SHARDS, CAP, BLOCK)
        upstream = tile_grad.astype(jnp.float32).reshape(TILE, SHARDS, CAP, BLOCK)
        alive_mask = alive[None, :, :, None]
        positive = jnp.maximum(gate_value, 0.0)
        gate_grad = (upstream * up_value * 2.0 * positive * alive_mask).astype(jnp.bfloat16)
        up_grad = (upstream * positive * positive * alive_mask).astype(jnp.bfloat16)
        partial_value = jnp.einsum("nsck,dsck->nsd", gate_grad.astype(jnp.float32), gate_cols.astype(jnp.float32))
        partial_value = partial_value + jnp.einsum("nsck,dsck->nsd", up_grad.astype(jnp.float32), up_cols.astype(jnp.float32))
        rounded = lax.optimization_barrier(partial_value.astype(jnp.bfloat16)).astype(jnp.float32)
        input_tile = jnp.sum(rounded, axis=1).astype(jnp.bfloat16)
        gate_piece = jnp.dot(tile_rows.T, gate_grad.reshape(TILE, SHARDS * CAP * BLOCK), preferred_element_type=jnp.float32)
        up_piece = jnp.dot(tile_rows.T, up_grad.reshape(TILE, SHARDS * CAP * BLOCK), preferred_element_type=jnp.float32)
        gate_piece = lax.optimization_barrier(gate_piece.astype(jnp.bfloat16)).astype(jnp.float32)
        up_piece = lax.optimization_barrier(up_piece.astype(jnp.bfloat16)).astype(jnp.float32)
        columns = ((shard_ids * BPS + picked)[:, :, None] * BLOCK + unit_ids[None, None, :]).reshape(-1).astype(jnp.int32)
        gate_total = gate_total.at[:, columns].add(gate_piece)
        up_total = up_total.at[:, columns].add(up_piece)
        return (gate_total, up_total), input_tile

    start = (jnp.zeros((D, FF), jnp.float32), jnp.zeros((D, FF), jnp.float32))
    inputs = (tokens.reshape(TILES, TILE, D), out_grad.reshape(TILES, TILE, SHARDS, CAP * BLOCK), active)
    (gate_total, up_total), input_tiles = lax.scan(one_tile, start, inputs)
    input_grad = input_tiles.reshape(TOKENS, D)
    return input_grad, gate_total.astype(jnp.bfloat16), up_total.astype(jnp.bfloat16)
```

```python
import functools

import jax
import jax.numpy as jnp
from jax import lax
from jax.experimental import pallas as pl
from jax.experimental.pallas import tpu as pltpu
from jax.sharding import PartitionSpec as P

BLOCK = 128
CHUNKS = 1
VMEM_BYTES = 60 * 1024 * 1024

f32 = jnp.float32
bf16 = jnp.bfloat16
VM = pl.BlockSpec(memory_space=pltpu.VMEM)
SM = pl.BlockSpec(memory_space=pltpu.SMEM)
ANY = pl.BlockSpec(memory_space=pl.ANY)


def params():
    return pltpu.CompilerParams(vmem_limit_bytes=VMEM_BYTES)


def cost(flops, moved):
    return pl.CostEstimate(flops=flops, bytes_accessed=moved, transcendentals=0)


def fetch_kernel(count, cap, blocks, picked, gate_ref, up_ref, out_ref, sems):
    def copies(q):
        made = []
        for slot in range(cap):
            block = jnp.minimum(picked[q * cap + slot], blocks - 1)
            columns = pl.ds(pl.multiple_of(block * BLOCK, BLOCK), BLOCK)
            for which, ref in enumerate((gate_ref, up_ref)):
                at = which * cap + slot
                made.append(
                    pltpu.make_async_copy(
                        ref.at[:, columns],
                        out_ref.at[q, :, pl.ds(at * BLOCK, BLOCK)],
                        sems.at[q, at],
                    )
                )
        return made

    started = [copy for q in range(count) for copy in copies(q)]
    for copy in started:
        copy.start()
    for copy in started:
        copy.wait()


def fetch_columns(picked, w_gate, w_up, count, cap, blocks):
    rows = w_gate.shape[0]
    width = 2 * cap * BLOCK
    return pl.pallas_call(
        functools.partial(fetch_kernel, count, cap, blocks),
        out_shape=jax.ShapeDtypeStruct((count, rows, width), bf16),
        in_specs=[SM, ANY, ANY],
        out_specs=VM,
        scratch_shapes=[pltpu.SemaphoreType.DMA((count, 2 * cap))],
        compiler_params=params(),
        cost_estimate=cost(0, 2 * count * rows * width * 2),
    )(picked, w_gate, w_up)


def tile_rows(own, other, core, dc, rows):
    if dc == 0:
        lanes = pl.ds(pl.multiple_of(core * rows, BLOCK), rows)
        return [ref[:, lanes] for ref in own]
    ref = other[dc - 1]
    return [ref[j] for j in range(ref.shape[0])]


def partial_kernel(dims, where, columns, *refs):
    Z, X, C, T, rows = dims
    step = T + C - 1
    pieces, outs = refs[: Z * X * step], refs[Z * X * step :]
    core = where[0]
    for dz in range(Z):
        for dx in range(X):
            chip = dz * X + dx
            mine = pieces[chip * step : (chip + 1) * step]
            for dc in range(C):
                left = jnp.concatenate(tile_rows(mine[:T], mine[T:], core, dc, rows), axis=0)
                value = jnp.dot(left, columns[chip * C + dc], preferred_element_type=f32)
                if dc == 0:
                    outs[dz * C][dx] = value
                else:
                    outs[dz * C + dc][dx] = value.astype(bf16)


def partials(where, columns, pieces, dims, tall):
    Z, X, C, T, rows = dims
    width = columns.shape[2]
    shapes = []
    for _ in range(Z):
        shapes.append(jax.ShapeDtypeStruct((X, tall, width), f32))
        shapes += [jax.ShapeDtypeStruct((X, tall, width), bf16)] * (C - 1)
    count = Z * X * C
    return pl.pallas_call(
        functools.partial(partial_kernel, dims),
        out_shape=shapes,
        in_specs=[SM] + [VM] * (1 + len(pieces)),
        out_specs=[VM] * len(shapes),
        compiler_params=params(),
        cost_estimate=cost(2 * count * tall * rows * width, count * rows * width * 2),
    )(where, columns, *pieces)


def part_kernel(dims, columns, *refs):
    Z, X, C, T, rows = dims
    grads, outs = refs[: Z * X * C], refs[Z * X * C :]
    for chip in range(Z * X):
        for dc in range(C):
            q = chip * C + dc
            value = lax.dot_general(
                grads[q][...],
                columns[q],
                (((1,), (1,)), ((), ())),
                preferred_element_type=f32,
            ).astype(bf16)
            short = value.shape[0] // T
            for j in range(T):
                outs[chip * T + j][dc] = value[j * short : (j + 1) * short]


def shard_parts(columns, grads, dims):
    Z, X, C, T, rows = dims
    tall, width = grads[0].shape
    shape = jax.ShapeDtypeStruct((C, tall // T, rows), bf16)
    count = Z * X * C
    return pl.pallas_call(
        functools.partial(part_kernel, dims),
        out_shape=[shape] * (Z * X * T),
        in_specs=[VM] * (1 + len(grads)),
        out_specs=[VM] * (Z * X * T),
        compiler_params=params(),
        cost_estimate=cost(2 * count * tall * rows * width, count * rows * width * 2),
    )(columns, *grads)


def weight_kernel(dims, cap, blocks, chunks, stripe, where, picked, before, last, *refs):
    Z, X, C, T, rows = dims
    count = Z * X * C
    step = T + C - 1
    per_chunk = Z * X * step
    pieces = refs[: chunks * per_chunk]
    grads = refs[chunks * per_chunk : chunks * (per_chunk + count)]
    outs = refs[chunks * (per_chunk + count) : chunks * (per_chunk + count) + 2]
    blank, totals, rounded, blank_sems, sems = refs[-5:]
    core = where[0]
    blank[...] = jnp.zeros(blank.shape, bf16)
    stripes = blocks * BLOCK // stripe
    clears = []
    for which in range(2):
        for s in range(stripes):
            clears.append(
                pltpu.make_async_copy(
                    blank,
                    outs[which].at[:, pl.ds(s * stripe, stripe)],
                    blank_sems.at[which, s],
                )
            )
    for copy in clears:
        copy.start()
    for q in range(count):
        chip, dc = q // C, q % C
        left, right = [], []
        for h in range(chunks):
            base = h * per_chunk + chip * step
            left += tile_rows(
                pieces[base : base + T], pieces[base + T : base + step], core, dc, rows
            )
            right.append(grads[h * count + q][...])
        value = lax.dot_general(
            jnp.concatenate(left, axis=0),
            jnp.concatenate(right, axis=0),
            (((0,), (0,)), ((), ())),
            preferred_element_type=f32,
        )
        value = value.astype(bf16).astype(f32)
        for slot in range(cap):
            at = q * cap + slot
            earlier = before[at]
            for which in range(2):
                lanes = slice((which * cap + slot) * BLOCK, (which * cap + slot + 1) * BLOCK)
                totals[which, at] = value[:, lanes]

            @pl.when(earlier >= 0)
            def _():
                for which in range(2):
                    totals[which, at] = totals[which, at] + totals[which, earlier]

            for which in range(2):
                rounded[which, at] = totals[which, at].astype(bf16)
    for copy in clears:
        copy.wait()

    def placing(which, at):
        block = jnp.minimum(picked[at], blocks - 1)
        return pltpu.make_async_copy(
            rounded.at[which, at],
            outs[which].at[:, pl.ds(pl.multiple_of(block * BLOCK, BLOCK), BLOCK)],
            sems.at[which, at],
        )

    for at in range(count * cap):

        @pl.when(last[at] > 0)
        def _(at=at):
            placing(0, at).start()
            placing(1, at).start()

    for at in range(count * cap):

        @pl.when(last[at] > 0)
        def _(at=at):
            placing(0, at).wait()
            placing(1, at).wait()


def weight_grads(where, picked, pieces, grads, dims, cap, blocks, chunks):
    Z, X, C, T, rows = dims
    count = Z * X * C
    slots = count * cap
    width = blocks * BLOCK
    stripe = width
    for parts in range(1, blocks + 1):
        if blocks % parts == 0 and rows * width // parts * 2 <= 4 << 20:
            stripe = width // parts
            break
    order = jnp.arange(slots, dtype=jnp.int32)
    live = picked < blocks
    same = (picked[:, None] == picked[None, :]) & live[:, None]
    before = jnp.max(jnp.where(same & (order[None, :] < order[:, None]), order[None, :], -1), axis=1)
    later = jnp.any(same & (order[None, :] > order[:, None]), axis=1)
    last = (live & ~later).astype(jnp.int32)
    out = jax.ShapeDtypeStruct((rows, width), bf16)
    tall = sum(g.shape[0] for g in grads[::count])
    return pl.pallas_call(
        functools.partial(weight_kernel, dims, cap, blocks, chunks, stripe),
        out_shape=[out, out],
        in_specs=[SM] * 4 + [VM] * (len(pieces) + len(grads)),
        out_specs=[ANY, ANY],
        scratch_shapes=[
            pltpu.VMEM((rows, stripe), bf16),
            pltpu.VMEM((2, slots, rows, BLOCK), f32),
            pltpu.VMEM((2, slots, rows, BLOCK), bf16),
            pltpu.SemaphoreType.DMA((2, width // stripe)),
            pltpu.SemaphoreType.DMA((2, slots)),
        ],
        compiler_params=params(),
        cost_estimate=cost(2 * count * tall * rows * 2 * cap * BLOCK, 2 * rows * width * 2),
    )(where, picked, before, last, *pieces, *grads)


def collect_kernel(dims, chips_in_shard, where, *refs):
    Z, X, C, T, rows = dims
    step = C
    pieces, outs = refs[: Z * X * step], refs[Z * X * step :]
    core, x, z, t = where[0], where[1], where[2], where[3]
    for dz in range(Z):
        for dx in range(X):
            chip = lax.rem(z + Z - dz, Z) * X + lax.rem(x + X - dx, X)
            shard = lax.div(chip, chips_in_shard)
            j = lax.rem(shard + T - t, T)
            for dc in range(C):
                ref = pieces[(dz * X + dx) * step + dc]
                value = ref[0] if dc == 0 else ref[...]
                start = (lax.rem(chip, chips_in_shard) * C + lax.rem(core + C - dc, C)) * rows
                lanes = pl.ds(pl.multiple_of(start, BLOCK), rows)
                for k in range(T):

                    @pl.when(j == k)
                    def _(k=k, value=value, lanes=lanes):
                        outs[k][:, lanes] = value


def collect(where, pieces, dims, chips_in_shard, features):
    Z, X, C, T, rows = dims
    short = pieces[0].shape[1]
    shape = jax.ShapeDtypeStruct((short, features), bf16)
    return pl.pallas_call(
        functools.partial(collect_kernel, dims, chips_in_shard),
        out_shape=[shape] * T,
        in_specs=[SM] + [VM] * len(pieces),
        out_specs=[VM] * T,
        compiler_params=params(),
        cost_estimate=cost(0, 2 * T * short * features * 2),
    )(where, *pieces)


def per_device(tokens, out_grad, active, w_gate, w_up):
    n, T = lax.axis_size("dp"), lax.axis_size("tensor")
    C = 2 if n % 2 == 0 else 1
    X = 2 if n % (2 * C) == 0 else 1
    Z = n // (C * X)
    height, features = tokens.shape
    rows = w_gate.shape[0]
    blocks = w_gate.shape[1] // BLOCK
    cap = active.shape[2]
    units = cap * BLOCK
    H = CHUNKS
    short = height // (T * H)
    tall = T * short
    chips_in_shard = (n // C) // T
    dims = (Z, X, C, T, rows)
    me, t = lax.axis_index("dp"), lax.axis_index("tensor")
    core, x, z = me % C, me // C % X, me // (C * X)
    where = jnp.stack([core, x, z, t]).astype(jnp.int32)

    def at(zi, xi, ci):
        return ((zi % Z) * X + xi % X) * C + ci % C

    def pull(v, dz, dx, dc):
        if dz % Z == 0 and dx % X == 0 and dc % C == 0:
            return v
        pairs = [
            (at(zi + dz, xi + dx, ci + dc), at(zi, xi, ci))
            for zi in range(Z)
            for xi in range(X)
            for ci in range(C)
        ]
        return lax.ppermute(v, "dp", pairs)

    def pull_t(v, j):
        if j % T == 0:
            return v
        return lax.ppermute(v, "tensor", [((i + j) % T, i) for i in range(T)])

    chips = [(dz, dx) for dz in range(Z) for dx in range(X)]

    listed = active.reshape(1, cap)
    listed = jnp.concatenate([pull(listed, 0, 0, dc) for dc in range(C)], axis=0)
    listed = jnp.concatenate([pull(listed, 0, dx, 0) for dx in range(X)], axis=0)
    listed = jnp.concatenate([pull(listed, dz, 0, 0) for dz in range(Z)], axis=0)
    picked = listed.reshape(n * cap)

    parts = tokens.reshape(T, H, short, features)

    def spread(h):
        shared = [lax.dynamic_index_in_dim(parts, t, 0, False)[h]]
        for j in range(1, T):
            sent = lax.dynamic_index_in_dim(parts, (t - j) % T, 0, False)[h]
            shared.append(pull_t(sent, j))
        shared = jnp.stack(shared)
        pieces = []
        for dz, dx in chips:
            chip = ((z - dz) % Z) * X + (x - dx) % X
            j = (chip // chips_in_shard - t) % T
            start = (chip % chips_in_shard) * (C * rows)
            sent = lax.dynamic_slice(shared, (j, 0, start), (1, short, C * rows))[0]
            got = pull(sent, dz, dx, 0)
            own = [pull_t(got, k) for k in range(T)]
            pieces += own
            for dc in range(1, C):
                start = ((core - dc) % C) * rows
                sent = jnp.stack([lax.dynamic_slice(v, (0, start), (short, rows)) for v in own])
                pieces.append(pull(sent, 0, 0, dc))
        return pieces

    def reduce_parts(out):
        summed = []
        for dz in range(Z):
            total = out[dz * C]
            for dc in range(1, C):
                total = total + pull(out[dz * C + dc], 0, 0, -dc).astype(f32)
            acc = total[0]
            for dx in range(1, X):
                acc = acc + pull(total[dx].astype(bf16), 0, -dx, 0).astype(f32)
            summed.append(acc)
        total = summed[0]
        for dz in range(1, Z):
            total = total + pull(summed[dz].astype(bf16), -dz, 0, 0).astype(f32)
        return total

    alive = (active.reshape(cap, 1) < blocks).astype(f32)
    alive = jnp.broadcast_to(alive, (cap, BLOCK)).reshape(1, units)
    upstream = out_grad.reshape(T, H, short, units)

    def grads_of(total, h):
        g = [lax.dynamic_index_in_dim(upstream, (t + j) % T, 0, False)[h] for j in range(T)]
        g = jnp.concatenate(g, axis=0).astype(f32)
        gate, up = total[:, :units], total[:, units:]
        positive = jnp.maximum(gate, 0.0)
        gate_grad = (g * up * 2.0 * positive * alive).astype(bf16)
        up_grad = (g * positive * positive * alive).astype(bf16)
        return jnp.concatenate([gate_grad, up_grad], axis=1)

    def gather_grads(mine):
        found = []
        for dz in range(Z):
            along_z = pull(mine, dz, 0, 0)
            for dx in range(X):
                along_x = pull(along_z, 0, dx, 0)
                found += [pull(along_x, 0, 0, dc) for dc in range(C)]
        return found

    def give_back(out):
        pieces = []
        for at_chip, (dz, dx) in enumerate(chips):
            mine = out[at_chip * T : (at_chip + 1) * T]
            total = mine[0].astype(f32)
            for j in range(1, T):
                total = total + pull_t(mine[j], -j).astype(f32)
            got = pull(total.astype(bf16), -dz, -dx, 0)
            pieces.append(got)
            pieces += [pull(got[dc], 0, 0, -dc) for dc in range(1, C)]
        held = collect(where, pieces, dims, chips_in_shard, features)
        return [pull_t(held[j], -j) for j in range(T)]

    columns = fetch_columns(picked, w_gate, w_up, n, cap, blocks)
    rows_of, grads = [], []
    for h in range(H):
        pieces = spread(h)
        rows_of.append(pieces)
        total = reduce_parts(partials(where, columns, pieces, dims, tall))
        grads.append(gather_grads(grads_of(total, h)))
    given = [give_back(shard_parts(columns, grads[h], dims)) for h in range(H)]
    gate_weight_grad, up_weight_grad = weight_grads(
        where, picked, sum(rows_of, []), sum(grads, []), dims, cap, blocks, H
    )
    input_grad = jnp.zeros((height, features), bf16)
    for h in range(H):
        for j in range(T):
            start = (((t - j) % T) * H + h) * short
            input_grad = lax.dynamic_update_slice(input_grad, given[h][j], (start, 0))
    return input_grad, gate_weight_grad, up_weight_grad


def solution(mesh):
    placed = (
        P("dp", "tensor"),
        P("dp", "tensor", None),
        P("dp", "tensor", None),
        P("dp", "tensor"),
        P("dp", "tensor"),
    )
    return jax.shard_map(
        per_device,
        mesh=mesh,
        in_specs=placed,
        out_specs=(P("dp", "tensor"), P("dp", "tensor"), P("dp", "tensor")),
        check_vma=False,
    )
```
